256 devices in a mesh: mode: 16 (over z, core), cols: 16 (over x, y).
Axes of the slice: x: 4, y: 4, z: 8, core: 2. Of those that a mesh axis runs over, the one named last changes fastest.
Arguments:
- snapshots: float32 [512, 262144], P('mode', 'cols'), may hold values from -54 to 54, as said below
- start_basis: float32 [512, 128], replicated, may hold values from -6 to 6
Outputs:
- subspace_basis: float32 [512, 128], replicated
- core_tensor: float32 [128, 262144], P('mode', 'cols')
The draws below stay inside these ranges and needn't reach their ends.
Inputs may be any that keep to these rules, and one draw needn't show every extreme that they name: `snapshots`: entries are finite real values.
All inputs are finite; a program needn't handle non-finite values.
Results may differ from the reference program's by a relative error of at most 0.00017.
Values sent between devices are 32-bit elements; how exact they have to be, the bound alone decides.
No kernel may reach another device: no remote copies, remote signals or barrier semaphores. Data moves between devices by JAX's collectives and lax.ppermute only.
A program may use at most 64 MiB of HBM per device.

```python
import math
import jax
import jax.numpy as jnp
from jax import lax

I1 = 512
RANK = 128
COLS = 262144


def draw_snapshots(key, part):
    key_base = jax.random.fold_in(key, 11)
    key_rows = jax.random.fold_in(key, 12)
    key_cols = jax.random.fold_in(key, 13)
    base_field = jnp.clip(jax.random.normal(key_base, (I1, COLS), jnp.float32), -6.0, 6.0)
    row_scale = jnp.exp(jax.random.uniform(key_rows, (I1,), jnp.float32) * math.log(16.0)) / 16.0
    ramp = 1.0 + 2.0 * jnp.arange(COLS, dtype=jnp.float32) / COLS
    col_scale = jnp.exp(jax.random.uniform(key_cols, (COLS,), jnp.float32) * math.log(3.0)) * ramp
    return base_field * row_scale[:, None] * col_scale[None, :]


def gaussian(own_key, extent, deviation, bound, held_as=jnp.bfloat16):
    entries = jax.random.normal(own_key, extent, jnp.float32) * deviation
    return jnp.minimum(jnp.maximum(entries, -bound), bound).astype(held_as)


def setup_inputs(seed: int = 0) -> dict:
    streams_of = jax.random.split(jax.random.key(seed), 3)
    return {
        "snapshots": draw_snapshots(jax.random.fold_in(streams_of[2], 71), 0),
        "start_basis": gaussian(streams_of[1], (I1, RANK), 1.0, 6.0, jnp.float32),
    }


def orthonormal(projected):
    current = projected
    for sweep in range(2):
        inner = jnp.dot(current.T.astype(jnp.float32), current.astype(jnp.float32), precision=lax.Precision.HIGHEST, preferred_element_type=jnp.float32)
        lower_part = jnp.linalg.cholesky(inner)
        current = jax.scipy.linalg.solve_triangular(lower_part, current.T, lower=True).T
    return current

def reference(snapshots, start_basis):
    gram_full = jnp.dot(snapshots.astype(jnp.float32), snapshots.T.astype(jnp.float32), precision=lax.Precision.HIGHEST, preferred_element_type=jnp.float32)
    factor = jnp.linalg.cholesky(gram_full)
    inner_step = jnp.dot(factor.T.astype(jnp.float32), start_basis.astype(jnp.float32), precision=lax.Precision.HIGHEST, preferred_element_type=jnp.float32)
    projected = jnp.dot(factor.astype(jnp.float32), inner_step.astype(jnp.float32), precision=lax.Precision.HIGHEST, preferred_element_type=jnp.float32)
    subspace_basis = orthonormal(projected)
    core_tensor = jnp.dot(subspace_basis.T.astype(jnp.float32), snapshots.astype(jnp.float32), precision=lax.Precision.HIGHEST, preferred_element_type=jnp.float32)
    return (subspace_basis, core_tensor)
```

```python
import jax
import jax.numpy as jnp
from jax import lax
from jax.experimental import pallas as pl
from jax.experimental.pallas import tpu as pltpu
from jax.sharding import Mesh
from jax.sharding import PartitionSpec as P

MODE = ("z", "core")
COLS = ("x", "y")
BLOCK = 8
LANES = 128


def spread(value):
    return jnp.broadcast_to(value, (BLOCK, LANES))


def exact_dot(left, right, dims):
    return lax.dot_general(
        left,
        right,
        (dims, ((), ())),
        precision=lax.Precision.HIGHEST,
        preferred_element_type=jnp.float32,
    )


def invert_factor(work):
    rank = work.shape[0]
    halves = (slice(0, rank), slice(rank, 2 * rank))
    for first in range(0, rank, BLOCK):
        rows = [
            [spread(work[first + i : first + i + 1, half]) for half in halves] for i in range(BLOCK)
        ]
        entry = {
            (i, j): spread(rows[i][0][:, first + j : first + j + 1])
            for i in range(BLOCK)
            for j in range(i + 1)
        }
        lower = {}
        inverse_pivot = []
        for j in range(BLOCK):
            inverse_pivot.append(lax.rsqrt(entry[j, j]))
            for i in range(j + 1, BLOCK):
                lower[i, j] = entry[i, j] * inverse_pivot[j]
            for i in range(j + 1, BLOCK):
                for m in range(i, BLOCK):
                    entry[m, i] = entry[m, i] - lower[m, j] * lower[i, j]
        solved = []
        for i in range(BLOCK):
            line = rows[i]
            for k in range(i):
                line = [part - lower[i, k] * known for part, known in zip(line, solved[k])]
            solved.append([part * inverse_pivot[i] for part in line])
            work[first + i : first + i + 1, halves[1]] = solved[i][1][:1]
        for later in range(first + BLOCK, rank, BLOCK):
            group = slice(later, later + BLOCK)
            left = work[group, halves[0]]
            right = work[group, halves[1]]
            columns = []
            for k in range(BLOCK):
                column = spread(left[:, first + k : first + k + 1])
                for m in range(k):
                    column = column - columns[m] * lower[k, m]
                columns.append(column * inverse_pivot[k])
            for k in range(BLOCK):
                left = left - columns[k] * solved[k][0]
                right = right - columns[k] * solved[k][1]
            work[group, halves[0]] = left
            work[group, halves[1]] = right


def orthonormal_kernel(projected, basis, work):
    rank = projected.shape[0]
    basis[...] = projected[...]

    def sweep(_, carry):
        current = basis[...]
        work[:, :rank] = exact_dot(current, current, ((1,), (1,)))
        across = lax.broadcasted_iota(jnp.int32, (rank, rank), 1)
        down = lax.broadcasted_iota(jnp.int32, (rank, rank), 0)
        work[:, rank:] = (across == down).astype(jnp.float32)
        invert_factor(work)
        basis[...] = exact_dot(work[:, rank:], current, ((1,), (0,)))
        return carry

    lax.fori_loop(0, 2, sweep, 0)


def orthonormal(projected):
    rank = projected.shape[0]
    return pl.pallas_call(
        orthonormal_kernel,
        out_shape=jax.ShapeDtypeStruct(projected.shape, jnp.float32),
        scratch_shapes=[pltpu.VMEM((rank, 2 * rank), jnp.float32)],
    )(projected)


def from_everyone(value, axis):
    copies = jnp.broadcast_to(value, (lax.axis_size(axis), *value.shape))
    return lax.all_to_all(copies, axis, split_axis=0, concat_axis=0, tiled=True)


def whole_sum(value):
    rows, lanes = value.shape
    tiles = value.reshape(rows // 8, 8, lanes // LANES, LANES).swapaxes(1, 2)
    halves = tiles.reshape(2, -1, 8, LANES)
    core = lax.axis_index("core")
    swap = [(0, 1), (1, 0)]
    away = lax.dynamic_index_in_dim(halves, 1 - core, 0, keepdims=False)
    kept = lax.dynamic_index_in_dim(halves, core, 0, keepdims=False)
    kept = kept + lax.ppermute(away, "core", swap)
    pieces = kept.reshape(lax.axis_size(COLS), -1, 8, LANES)
    own = lax.all_to_all(pieces, COLS, 0, 0, tiled=True).sum(axis=0)
    own = from_everyone(own, "z").sum(axis=0)
    half = from_everyone(own, COLS).reshape(kept.shape)
    other = lax.ppermute(half, "core", swap)
    first = core == 0
    joined = jnp.stack([jnp.where(first, half, other), jnp.where(first, other, half)])
    return joined.reshape(rows // 8, lanes // LANES, 8, LANES).swapaxes(1, 2).reshape(rows, lanes)


def shards(snapshots, start_basis):
    fibres = lax.all_to_all(snapshots, MODE, split_axis=1, concat_axis=0, tiled=True)
    along_cols = exact_dot(start_basis, fibres, ((0,), (0,)))
    partial_term = exact_dot(along_cols, fibres, ((1,), (1,)))
    basis = orthonormal(whole_sum(partial_term))
    core_local = exact_dot(basis, fibres, ((1,), (0,)))
    core_tensor = lax.all_to_all(core_local, MODE, split_axis=0, concat_axis=1, tiled=True)
    return (basis.T, core_tensor)


def solution(mesh):
    finer = Mesh(mesh.devices.reshape(8, 2, 4, 4), ("z", "core", "x", "y"))
    return jax.shard_map(
        shards,
        mesh=finer,
        in_specs=(P(MODE, COLS), P()),
        out_specs=(P(), P(MODE, COLS)),
        check_vma=False,
    )
```

```python
import jax
import jax.numpy as jnp
from jax import lax
from jax.experimental import pallas as pl
from jax.experimental.pallas import tpu as pltpu
from jax.sharding import Mesh
from jax.sharding import PartitionSpec as P

MODE = ("z", "core")
COLS = ("x", "y")
BLOCK = 8
PANEL = 64
CHUNK = 256
LANES = 128


def spread(value):
    return jnp.broadcast_to(value, (BLOCK, LANES))


def exact_dot(left, right, dims):
    return lax.dot_general(
        left,
        right,
        (dims, ((), ())),
        precision=lax.Precision.HIGHEST,
        preferred_element_type=jnp.float32,
    )


def close_dot(left, right, dims):
    return lax.dot_general(
        left,
        right,
        (dims, ((), ())),
        precision=lax.Precision.HIGH,
        preferred_element_type=jnp.float32,
    )


def two_terms(value):
    high = value.astype(jnp.bfloat16)
    return high, (value - high.astype(jnp.float32)).astype(jnp.bfloat16)


def three_products(left, right):
    left_high, left_low = left
    right_high, right_low = right
    small = jnp.dot(left_low, right_high, preferred_element_type=jnp.float32)
    small += jnp.dot(left_high, right_low, preferred_element_type=jnp.float32)
    return small + jnp.dot(left_high, right_high, preferred_element_type=jnp.float32)


def invert_factor(work, columns):
    rank = work.shape[0]
    lane = lax.broadcasted_iota(jnp.int32, (BLOCK, LANES), 1)
    for start in range(0, rank, PANEL):
        stop = start + PANEL
        for first in range(start, stop, BLOCK):
            lines = [spread(work[first + i : first + i + 1, :]) for i in range(BLOCK)]
            tile = work[first : first + BLOCK, :]
            for j in range(BLOCK):
                columns[BLOCK * j : BLOCK * (j + 1), :] = spread(tile[:, first + j : first + j + 1])
            entry = {
                (i, j): spread(columns[BLOCK * j + i : BLOCK * j + i + 1, :])
                for i in range(BLOCK)
                for j in range(i + 1)
            }
            inside = (lane >= first) & (lane < first + BLOCK)
            lines = [
                jnp.where(inside, (lane == first + i).astype(jnp.float32), line)
                for i, line in enumerate(lines)
            ]
            lower = {}
            inverse_pivot = []
            solved = []
            for j in range(BLOCK):
                inverse_pivot.append(lax.rsqrt(entry[j, j]))
                for i in range(j + 1, BLOCK):
                    lower[i, j] = entry[i, j] * inverse_pivot[j]
                for i in range(j + 1, BLOCK):
                    for m in range(i, BLOCK):
                        entry[m, i] = entry[m, i] - lower[m, j] * lower[i, j]
                solved.append(lines[j] * inverse_pivot[j])
                for i in range(j + 1, BLOCK):
                    lines[i] = lines[i] - lower[i, j] * solved[j]
                work[first + j : first + j + 1, :] = solved[j][:1]
            for later in range(first + BLOCK, stop, BLOCK):
                group = work[later : later + BLOCK, :]
                column = [spread(group[:, first + k : first + k + 1]) for k in range(BLOCK)]
                group = jnp.where(inside, 0.0, group)
                for k in range(BLOCK):
                    scaled = column[k] * inverse_pivot[k]
                    for m in range(k + 1, BLOCK):
                        column[m] = column[m] - scaled * lower[m, k]
                    group = group - scaled * solved[k]
                work[later : later + BLOCK, :] = group
        if stop < rank:
            panel = work[start:stop, :]
            across = lax.broadcasted_iota(jnp.int32, panel.shape, 1)
            down = lax.broadcasted_iota(jnp.int32, panel.shape, 0) + start
            known = jnp.where((across < stop) & (across > down), 0.0, panel)
            update = exact_dot(panel, known, ((0,), (0,)))
            rest = work[stop:, :]
            across = lax.broadcasted_iota(jnp.int32, rest.shape, 1)
            rest = jnp.where((across >= start) & (across < stop), 0.0, rest)
            work[stop:, :] = rest - update[stop:, :]


def finish_kernel(projected, fibres, basis, core, current, work, columns, whole, arrived):
    fetch = pltpu.make_async_copy(fibres, whole, arrived)
    fetch.start()
    current[...] = projected[...]

    def sweep(_, carry):
        before = current[...]
        work[...] = exact_dot(before, before, ((1,), (1,)))
        invert_factor(work, columns)
        across = lax.broadcasted_iota(jnp.int32, work.shape, 1)
        down = lax.broadcasted_iota(jnp.int32, work.shape, 0)
        inverse = jnp.where(across <= down, work[...], 0.0)
        current[...] = exact_dot(inverse, before, ((1,), (0,)))
        return carry

    lax.fori_loop(0, 2, sweep, 0)
    fetch.wait()
    rows = two_terms(current[...])
    for first in range(0, whole.shape[1], CHUNK):
        part = slice(first, first + CHUNK)
        core[:, part] = three_products(rows, two_terms(whole[:, part]))
    basis[...] = current[...].T


def finish(projected, fibres):
    rank, length = projected.shape
    some = fibres.shape[1]
    return pl.pallas_call(
        finish_kernel,
        out_shape=(
            jax.ShapeDtypeStruct((length, rank), jnp.float32),
            jax.ShapeDtypeStruct((rank, some), jnp.float32),
        ),
        in_specs=[pl.BlockSpec(memory_space=pltpu.VMEM), pl.BlockSpec(memory_space=pl.ANY)],
        scratch_shapes=[
            pltpu.VMEM((rank, length), jnp.float32),
            pltpu.VMEM((rank, rank), jnp.float32),
            pltpu.VMEM((BLOCK * BLOCK, LANES), jnp.float32),
            pltpu.VMEM(fibres.shape, jnp.float32),
            pltpu.SemaphoreType.DMA,
        ],
    )(projected, fibres)


def from_everyone(value, axis):
    copies = jnp.broadcast_to(value, (lax.axis_size(axis), *value.shape))
    return lax.all_to_all(copies, axis, split_axis=0, concat_axis=0, tiled=True)


def whole_sum(value):
    rows, lanes = value.shape
    tiles = value.reshape(rows // 8, 8, lanes // LANES, LANES).swapaxes(1, 2)
    near = ("core",) + COLS
    pieces = tiles.reshape(lax.axis_size(near), -1, 8, LANES)
    own = lax.all_to_all(pieces, near, 0, 0, tiled=True).sum(axis=0)
    own = from_everyone(own, "z").sum(axis=0)
    full = from_everyone(own, near)
    return full.reshape(rows // 8, lanes // LANES, 8, LANES).swapaxes(1, 2).reshape(rows, lanes)


def shards(snapshots, start_basis):
    fibres = lax.all_to_all(snapshots, MODE, split_axis=1, concat_axis=0, tiled=True)
    along_cols = close_dot(start_basis, fibres, ((0,), (0,)))
    partial_term = close_dot(along_cols, fibres, ((1,), (1,)))
    basis, core_local = finish(whole_sum(partial_term), fibres)
    core_tensor = lax.all_to_all(core_local, MODE, split_axis=0, concat_axis=1, tiled=True)
    return (basis, core_tensor)


def solution(mesh):
    finer = Mesh(mesh.devices.reshape(8, 2, 4, 4), ("z", "core", "x", "y"))
    return jax.shard_map(
        shards,
        mesh=finer,
        in_specs=(P(MODE, COLS), P()),
        out_specs=(P(), P(MODE, COLS)),
        check_vma=False,
    )
```

```python
import jax
import jax.numpy as jnp
from jax import lax
from jax.experimental import pallas as pl
from jax.experimental.pallas import tpu as pltpu
from jax.sharding import Mesh
from jax.sharding import PartitionSpec as P

MODE = ("z", "core")
COLS = ("x", "y")
BLOCK = 8
PANEL = 64
CHUNK = 256
LANES = 128


def spread(value):
    return jnp.broadcast_to(value, (BLOCK, LANES))


def exact_dot(left, right, dims):
    return lax.dot_general(
        left,
        right,
        (dims, ((), ())),
        precision=lax.Precision.HIGHEST,
        preferred_element_type=jnp.float32,
    )


def close_dot(left, right, dims):
    return lax.dot_general(
        left,
        right,
        (dims, ((), ())),
        precision=lax.Precision.HIGH,
        preferred_element_type=jnp.float32,
    )


def two_terms(value):
    high = value.astype(jnp.bfloat16)
    return high, (value - high.astype(jnp.float32)).astype(jnp.bfloat16)


def three_products(left, right, dims=((1,), (0,))):
    def product(one, other):
        return lax.dot_general(one, other, (dims, ((), ())), preferred_element_type=jnp.float32)

    left_high, left_low = left
    right_high, right_low = right
    small = product(left_low, right_high) + product(left_high, right_low)
    return small + product(left_high, right_high)


def invert_factor(work, columns):
    rank = work.shape[0]
    lane = lax.broadcasted_iota(jnp.int32, (BLOCK, LANES), 1)
    for start in range(0, rank, PANEL):
        stop = start + PANEL
        for first in range(start, stop, BLOCK):
            lines = [spread(work[first + i : first + i + 1, :]) for i in range(BLOCK)]
            tile = work[first : first + BLOCK, :]
            for j in range(BLOCK):
                columns[BLOCK * j : BLOCK * (j + 1), :] = spread(tile[:, first + j : first + j + 1])
            entry = {
                (i, j): spread(columns[BLOCK * j + i : BLOCK * j + i + 1, :])
                for i in range(BLOCK)
                for j in range(i + 1)
            }
            inside = (lane >= first) & (lane < first + BLOCK)
            lines = [
                jnp.where(inside, (lane == first + i).astype(jnp.float32), line)
                for i, line in enumerate(lines)
            ]
            lower = {}
            inverse_pivot = []
            solved = []
            for j in range(BLOCK):
                inverse_pivot.append(lax.rsqrt(entry[j, j]))
                for i in range(j + 1, BLOCK):
                    lower[i, j] = entry[i, j] * inverse_pivot[j]
                for i in range(j + 1, BLOCK):
                    for m in range(i, BLOCK):
                        entry[m, i] = entry[m, i] - lower[m, j] * lower[i, j]
                solved.append(lines[j] * inverse_pivot[j])
                for i in range(j + 1, BLOCK):
                    lines[i] = lines[i] - lower[i, j] * solved[j]
                work[first + j : first + j + 1, :] = solved[j][:1]
            for later in range(first + BLOCK, stop, BLOCK):
                group = work[later : later + BLOCK, :]
                column = [spread(group[:, first + k : first + k + 1]) for k in range(BLOCK)]
                group = jnp.where(inside, 0.0, group)
                for k in range(BLOCK):
                    scaled = column[k] * inverse_pivot[k]
                    for m in range(k + 1, BLOCK):
                        column[m] = column[m] - scaled * lower[m, k]
                    group = group - scaled * solved[k]
                work[later : later + BLOCK, :] = group
        if stop < rank:
            panel = work[start:stop, :]
            across = lax.broadcasted_iota(jnp.int32, panel.shape, 1)
            down = lax.broadcasted_iota(jnp.int32, panel.shape, 0) + start
            known = jnp.where((across < stop) & (across > down), 0.0, panel)
            update = three_products(two_terms(panel), two_terms(known), ((0,), (0,)))
            rest = work[stop:, :]
            across = lax.broadcasted_iota(jnp.int32, rest.shape, 1)
            rest = jnp.where((across >= start) & (across < stop), 0.0, rest)
            work[stop:, :] = rest - update[stop:, :]


def finish_kernel(place, own, other, fibres, basis, core, current, work, columns):
    rows = own.shape[0]
    first = place[0] == 0
    current[:rows, :] = jnp.where(first, own[...], other[...])
    current[rows:, :] = jnp.where(first, other[...], own[...])

    def sweep(_, carry):
        before = current[...]
        terms = two_terms(before)
        work[...] = three_products(terms, terms, ((1,), (1,)))
        invert_factor(work, columns)
        across = lax.broadcasted_iota(jnp.int32, work.shape, 1)
        down = lax.broadcasted_iota(jnp.int32, work.shape, 0)
        inverse = jnp.where(across <= down, work[...], 0.0)
        current[...] = exact_dot(inverse, before, ((1,), (0,)))
        return carry

    lax.fori_loop(0, 2, sweep, 0)
    rows = two_terms(current[...])
    for first in range(0, fibres.shape[1], CHUNK):
        part = slice(first, first + CHUNK)
        core[:, part] = three_products(rows, two_terms(fibres[:, part]))
    basis[...] = current[...].T


def in_vmem(value):
    return pltpu.with_memory_space_constraint(value, pltpu.VMEM)


def finish(core, own, other, fibres):
    rank, length = own.shape[0] * 2, own.shape[1]
    some = fibres.shape[1]
    return pl.pallas_call(
        finish_kernel,
        out_shape=(
            jax.ShapeDtypeStruct((length, rank), jnp.float32),
            pltpu.VMEM((rank, some), jnp.float32),
        ),
        in_specs=[
            pl.BlockSpec(memory_space=pltpu.SMEM),
            pl.BlockSpec(memory_space=pltpu.VMEM),
            pl.BlockSpec(memory_space=pltpu.VMEM),
            pl.BlockSpec(memory_space=pltpu.VMEM),
        ],
        out_specs=(pl.BlockSpec(memory_space=pltpu.VMEM), pl.BlockSpec(memory_space=pltpu.VMEM)),
        scratch_shapes=[
            pltpu.VMEM((rank, length), jnp.float32),
            pltpu.VMEM((rank, rank), jnp.float32),
            pltpu.VMEM((BLOCK * BLOCK, LANES), jnp.float32),
        ],
        compiler_params=pltpu.CompilerParams(vmem_limit_bytes=16 * 2**20),
    )(
        core[None], in_vmem(own), in_vmem(other), in_vmem(fibres)
    )


def regroup_kernel(snapshots, pieces, arrived):
    members, _, some = pieces.shape
    arrivals = []
    for member in range(members):
        columns = slice(member * some, (member + 1) * some)
        arrivals.append(
            pltpu.make_async_copy(snapshots.at[:, columns], pieces.at[member], arrived.at[member])
        )
        arrivals[-1].start()
    for arrival in arrivals:
        arrival.wait()


def regroup(snapshots, members):
    rows, length = snapshots.shape
    return pl.pallas_call(
        regroup_kernel,
        out_shape=pltpu.VMEM((members, rows, length // members), jnp.float32),
        in_specs=[pl.BlockSpec(memory_space=pl.ANY)],
        out_specs=pl.BlockSpec(memory_space=pltpu.VMEM),
        scratch_shapes=[pltpu.SemaphoreType.DMA((members,))],
        compiler_params=pltpu.CompilerParams(vmem_limit_bytes=4 * 2**20),
    )(pltpu.with_memory_space_constraint(snapshots, pltpu.HBM))


def from_everyone(value, axis):
    copies = jnp.broadcast_to(value, (lax.axis_size(axis), *value.shape))
    return lax.all_to_all(copies, axis, split_axis=0, concat_axis=0, tiled=True)


def half_sums(value, core):
    rows, lanes = value.shape
    tiles = value.reshape(rows // 8, 8, lanes // LANES, LANES).swapaxes(1, 2)
    halves = tiles.reshape(2, -1, 8, LANES)
    swap = [(0, 1), (1, 0)]
    away = lax.dynamic_index_in_dim(halves, 1 - core, 0, keepdims=False)
    kept = lax.dynamic_index_in_dim(halves, core, 0, keepdims=False)
    kept = kept + lax.ppermute(away, "core", swap)
    pieces = kept.reshape(lax.axis_size(COLS), -1, 8, LANES)
    own = lax.all_to_all(pieces, COLS, 0, 0, tiled=True).sum(axis=0)
    own = from_everyone(own, "z").sum(axis=0)
    half = from_everyone(own, COLS)
    other = lax.ppermute(half, "core", swap)
    shape = (rows // 16, lanes // LANES, 8, LANES)
    return [
        part.reshape(shape).swapaxes(1, 2).reshape(rows // 2, lanes) for part in (half, other)
    ]


def shards(snapshots, start_basis):
    pieces = regroup(snapshots, lax.axis_size(MODE))
    core = lax.axis_index("core")
    pieces, core = lax.optimization_barrier((pieces, core))
    fibres = lax.all_to_all(pieces, MODE, 0, 0, tiled=True)
    fibres = fibres.reshape(-1, fibres.shape[-1])
    fibres, start_basis, core = lax.optimization_barrier((fibres, start_basis, core))
    along_cols = close_dot(start_basis, fibres, ((0,), (0,)))
    partial_term = close_dot(along_cols, fibres, ((1,), (1,)))
    basis, core_local = finish(core, *half_sums(partial_term, core), fibres)
    core_tensor = lax.all_to_all(core_local, MODE, split_axis=0, concat_axis=1, tiled=True)
    return (basis, core_tensor)


def solution(mesh):
    finer = Mesh(mesh.devices.reshape(8, 2, 4, 4), ("z", "core", "x", "y"))
    return jax.shard_map(
        shards,
        mesh=finer,
        in_specs=(P(MODE, COLS), P()),
        out_specs=(P(), P(MODE, COLS)),
        check_vma=False,
    )
```

```python
import jax
import jax.numpy as jnp
from jax import lax
from jax.experimental import pallas as pl
from jax.experimental.pallas import tpu as pltpu
from jax.sharding import Mesh
from jax.sharding import PartitionSpec as P

MODE = ("z", "core")
COLS = ("x", "y")
BLOCK = 8
PANEL = 64
CHUNK = 256
LANES = 128


def spread(value):
    return jnp.broadcast_to(value, (BLOCK, LANES))


def exact_dot(left, right, dims):
    return lax.dot_general(
        left,
        right,
        (dims, ((), ())),
        precision=lax.Precision.HIGHEST,
        preferred_element_type=jnp.float32,
    )


def close_dot(left, right, dims):
    return lax.dot_general(
        left,
        right,
        (dims, ((), ())),
        precision=lax.Precision.HIGH,
        preferred_element_type=jnp.float32,
    )


def two_terms(value):
    high = value.astype(jnp.bfloat16)
    return high, (value - high.astype(jnp.float32)).astype(jnp.bfloat16)


def three_products(left, right, dims=((1,), (0,))):
    def product(one, other):
        return lax.dot_general(one, other, (dims, ((), ())), preferred_element_type=jnp.float32)

    left_high, left_low = left
    right_high, right_low = right
    small = product(left_low, right_high) + product(left_high, right_low)
    return small + product(left_high, right_high)


def invert_factor(work, columns):
    rank = work.shape[0]
    lane = lax.broadcasted_iota(jnp.int32, (BLOCK, LANES), 1)
    for start in range(0, rank, PANEL):
        stop = start + PANEL
        for first in range(start, stop, BLOCK):
            lines = [spread(work[first + i : first + i + 1, :]) for i in range(BLOCK)]
            tile = work[first : first + BLOCK, :]
            for j in range(BLOCK):
                columns[BLOCK * j : BLOCK * (j + 1), :] = spread(tile[:, first + j : first + j + 1])
            entry = {
                (i, j): spread(columns[BLOCK * j + i : BLOCK * j + i + 1, :])
                for i in range(BLOCK)
                for j in range(i + 1)
            }
            inside = (lane >= first) & (lane < first + BLOCK)
            lines = [
                jnp.where(inside, (lane == first + i).astype(jnp.float32), line)
                for i, line in enumerate(lines)
            ]
            lower = {}
            inverse_pivot = []
            solved = []
            for j in range(0, BLOCK, 2):
                determinant = entry[j, j] * entry[j + 1, j + 1] - entry[j + 1, j] * entry[j + 1, j]
                inverse_pivot.append(lax.rsqrt(entry[j, j]))
                root = entry[j, j] * inverse_pivot[j]
                inverse_pivot.append(lax.rsqrt(determinant) * root)
                lower[j + 1, j] = entry[j + 1, j] * inverse_pivot[j]
                for i in range(j + 2, BLOCK):
                    lower[i, j] = entry[i, j] * inverse_pivot[j]
                    rest = entry[i, j + 1] - lower[i, j] * lower[j + 1, j]
                    lower[i, j + 1] = rest * inverse_pivot[j + 1]
                for i in range(j + 2, BLOCK):
                    for m in range(i, BLOCK):
                        for k in (j, j + 1):
                            entry[m, i] = entry[m, i] - lower[m, k] * lower[i, k]
                for k in (j, j + 1):
                    solved.append(lines[k] * inverse_pivot[k])
                    for i in range(k + 1, BLOCK):
                        lines[i] = lines[i] - lower[i, k] * solved[k]
                    work[first + k : first + k + 1, :] = solved[k][:1]
            for later in range(first + BLOCK, stop, BLOCK):
                group = work[later : later + BLOCK, :]
                column = [spread(group[:, first + k : first + k + 1]) for k in range(BLOCK)]
                group = jnp.where(inside, 0.0, group)
                for k in range(BLOCK):
                    scaled = column[k] * inverse_pivot[k]
                    for m in range(k + 1, BLOCK):
                        column[m] = column[m] - scaled * lower[m, k]
                    group = group - scaled * solved[k]
                work[later : later + BLOCK, :] = group
        if stop < rank:
            panel = work[start:stop, :]
            across = lax.broadcasted_iota(jnp.int32, panel.shape, 1)
            down = lax.broadcasted_iota(jnp.int32, panel.shape, 0) + start
            known = jnp.where((across < stop) & (across > down), 0.0, panel)
            update = three_products(two_terms(panel), two_terms(known), ((0,), (0,)))
            rest = work[stop:, :]
            across = lax.broadcasted_iota(jnp.int32, rest.shape, 1)
            rest = jnp.where((across >= start) & (across < stop), 0.0, rest)
            work[stop:, :] = rest - update[stop:, :]


def finish_kernel(
    place, own, other, fibres, basis, core, current, work, columns, turned, left
):
    rows = own.shape[0]
    first = place[0] == 0
    current[:rows, :] = jnp.where(first, own[...], other[...])
    current[rows:, :] = jnp.where(first, other[...], own[...])
    for top in range(0, current.shape[0], BLOCK):
        some = current[top : top + BLOCK, :]
        current[top : top + BLOCK, :] = some * lax.rsqrt(jnp.sum(some * some, axis=1, keepdims=True))

    def sweep(_, carry):
        before = current[...]
        terms = two_terms(before)
        work[...] = three_products(terms, terms, ((1,), (1,)))
        invert_factor(work, columns)
        across = lax.broadcasted_iota(jnp.int32, work.shape, 1)
        down = lax.broadcasted_iota(jnp.int32, work.shape, 0)
        inverse = jnp.where(across <= down, work[...], 0.0)
        current[...] = exact_dot(inverse, before, ((1,), (0,)))
        return carry

    lax.fori_loop(0, 2, sweep, 0)
    turned[...] = current[...].T
    send = pltpu.make_async_copy(turned, basis, left)
    send.start()
    rows = two_terms(current[...])
    for first in range(0, fibres.shape[1], CHUNK):
        part = slice(first, first + CHUNK)
        core[:, part] = three_products(rows, two_terms(fibres[:, part]))
    send.wait()


def in_vmem(value):
    return pltpu.with_memory_space_constraint(value, pltpu.VMEM)


def finish(core, own, other, fibres):
    rank, length = own.shape[0] * 2, own.shape[1]
    some = fibres.shape[1]
    return pl.pallas_call(
        finish_kernel,
        out_shape=(
            pltpu.HBM((length, rank), jnp.float32),
            pltpu.VMEM((rank, some), jnp.float32),
        ),
        in_specs=[
            pl.BlockSpec(memory_space=pltpu.SMEM),
            pl.BlockSpec(memory_space=pltpu.VMEM),
            pl.BlockSpec(memory_space=pltpu.VMEM),
            pl.BlockSpec(memory_space=pltpu.VMEM),
        ],
        out_specs=(pl.BlockSpec(memory_space=pl.ANY), pl.BlockSpec(memory_space=pltpu.VMEM)),
        scratch_shapes=[
            pltpu.VMEM((rank, length), jnp.float32),
            pltpu.VMEM((rank, rank), jnp.float32),
            pltpu.VMEM((BLOCK * BLOCK, LANES), jnp.float32),
            pltpu.VMEM((length, rank), jnp.float32),
            pltpu.SemaphoreType.DMA,
        ],
        compiler_params=pltpu.CompilerParams(vmem_limit_bytes=16 * 2**20),
    )(
        core[None], in_vmem(own), in_vmem(other), in_vmem(fibres)
    )


def regroup_kernel(snapshots, pieces, arrived):
    members, _, some = pieces.shape
    arrivals = []
    for member in range(members):
        columns = slice(member * some, (member + 1) * some)
        arrivals.append(
            pltpu.make_async_copy(snapshots.at[:, columns], pieces.at[member], arrived.at[member])
        )
        arrivals[-1].start()
    for arrival in arrivals:
        arrival.wait()


def regroup(snapshots, members):
    rows, length = snapshots.shape
    return pl.pallas_call(
        regroup_kernel,
        out_shape=pltpu.VMEM((members, rows, length // members), jnp.float32),
        in_specs=[pl.BlockSpec(memory_space=pl.ANY)],
        out_specs=pl.BlockSpec(memory_space=pltpu.VMEM),
        scratch_shapes=[pltpu.SemaphoreType.DMA((members,))],
        compiler_params=pltpu.CompilerParams(vmem_limit_bytes=4 * 2**20),
    )(pltpu.with_memory_space_constraint(snapshots, pltpu.HBM))


def from_everyone(value, axis):
    copies = jnp.broadcast_to(value, (lax.axis_size(axis), *value.shape))
    return lax.all_to_all(copies, axis, split_axis=0, concat_axis=0, tiled=True)


def half_sums(value, core):
    rows, lanes = value.shape
    tiles = value.reshape(rows // 8, 8, lanes // LANES, LANES).swapaxes(1, 2)
    halves = tiles.reshape(2, -1, 8, LANES)
    swap = [(0, 1), (1, 0)]
    away = lax.dynamic_index_in_dim(halves, 1 - core, 0, keepdims=False)
    kept = lax.dynamic_index_in_dim(halves, core, 0, keepdims=False)
    kept = kept + lax.ppermute(away, "core", swap)
    pieces = kept.reshape(lax.axis_size(COLS), -1, 8, LANES)
    own = lax.all_to_all(pieces, COLS, 0, 0, tiled=True).sum(axis=0)
    own = from_everyone(own, "z").sum(axis=0)
    half = from_everyone(own, COLS)
    other = lax.ppermute(half, "core", swap)
    shape = (rows // 16, lanes // LANES, 8, LANES)
    return [
        part.reshape(shape).swapaxes(1, 2).reshape(rows // 2, lanes) for part in (half, other)
    ]


def shards(snapshots, start_basis):
    pieces = regroup(snapshots, lax.axis_size(MODE))
    core = lax.axis_index("core")
    pieces, core = lax.optimization_barrier((pieces, core))
    fibres = lax.all_to_all(pieces, MODE, 0, 0, tiled=True)
    fibres = fibres.reshape(-1, fibres.shape[-1])
    fibres, start_basis, core = lax.optimization_barrier((fibres, start_basis, core))
    along_cols = close_dot(start_basis, fibres, ((0,), (0,)))
    partial_term = close_dot(along_cols, fibres, ((1,), (1,)))
    basis, core_local = finish(core, *half_sums(partial_term, core), fibres)
    core_tensor = lax.all_to_all(core_local, MODE, split_axis=0, concat_axis=1, tiled=True)
    return (basis, core_tensor)


def solution(mesh):
    finer = Mesh(mesh.devices.reshape(8, 2, 4, 4), ("z", "core", "x", "y"))
    return jax.shard_map(
        shards,
        mesh=finer,
        in_specs=(P(MODE, COLS), P()),
        out_specs=(P(), P(MODE, COLS)),
        check_vma=False,
    )
```

```python
import jax
import jax.numpy as jnp
from jax import lax
from jax.experimental import pallas as pl
from jax.experimental.pallas import tpu as pltpu
from jax.sharding import Mesh
from jax.sharding import PartitionSpec as P

MODE = ("z", "core")
COLS = ("x", "y")
BLOCK = 8
PANEL = 64
CHUNK = 256
LANES = 128


def spread(value):
    return jnp.broadcast_to(value, (BLOCK, LANES))


def exact_dot(left, right, dims):
    return lax.dot_general(
        left,
        right,
        (dims, ((), ())),
        precision=lax.Precision.HIGHEST,
        preferred_element_type=jnp.float32,
    )


def close_dot(left, right, dims):
    return lax.dot_general(
        left,
        right,
        (dims, ((), ())),
        precision=lax.Precision.HIGH,
        preferred_element_type=jnp.float32,
    )


def two_terms(value):
    high = value.astype(jnp.bfloat16)
    return high, (value - high.astype(jnp.float32)).astype(jnp.bfloat16)


def three_products(left, right, dims=((1,), (0,))):
    def product(one, other):
        return lax.dot_general(one, other, (dims, ((), ())), preferred_element_type=jnp.float32)

    left_high, left_low = left
    right_high, right_low = right
    small = product(left_low, right_high) + product(left_high, right_low)
    return small + product(left_high, right_high)


def invert_factor(work, columns):
    rank = work.shape[0]
    lane = lax.broadcasted_iota(jnp.int32, (BLOCK, LANES), 1)
    for start in range(0, rank, PANEL):
        stop = start + PANEL
        for first in range(start, stop, BLOCK):
            lines = [spread(work[first + i : first + i + 1, :]) for i in range(BLOCK)]
            tile = work[first : first + BLOCK, :]
            for j in range(BLOCK):
                columns[BLOCK * j : BLOCK * (j + 1), :] = spread(tile[:, first + j : first + j + 1])
            entry = {
                (i, j): spread(columns[BLOCK * j + i : BLOCK * j + i + 1, :])
                for i in range(BLOCK)
                for j in range(i + 1)
            }
            inside = (lane >= first) & (lane < first + BLOCK)
            lines = [
                jnp.where(inside, (lane == first + i).astype(jnp.float32), line)
                for i, line in enumerate(lines)
            ]
            lower = {}
            inverse_pivot = []
            solved = []
            for j in range(0, BLOCK, 2):
                determinant = entry[j, j] * entry[j + 1, j + 1] - entry[j + 1, j] * entry[j + 1, j]
                inverse_pivot.append(lax.rsqrt(entry[j, j]))
                root = entry[j, j] * inverse_pivot[j]
                inverse_pivot.append(lax.rsqrt(determinant) * root)
                lower[j + 1, j] = entry[j + 1, j] * inverse_pivot[j]
                for i in range(j + 2, BLOCK):
                    lower[i, j] = entry[i, j] * inverse_pivot[j]
                    rest = entry[i, j + 1] - lower[i, j] * lower[j + 1, j]
                    lower[i, j + 1] = rest * inverse_pivot[j + 1]
                for i in range(j + 2, BLOCK):
                    for m in range(i, BLOCK):
                        for k in (j, j + 1):
                            entry[m, i] = entry[m, i] - lower[m, k] * lower[i, k]
                for k in (j, j + 1):
                    solved.append(lines[k] * inverse_pivot[k])
                    for i in range(k + 1, BLOCK):
                        lines[i] = lines[i] - lower[i, k] * solved[k]
                    work[first + k : first + k + 1, :] = solved[k][:1]
            for later in range(first + BLOCK, stop, BLOCK):
                group = work[later : later + BLOCK, :]
                column = [spread(group[:, first + k : first + k + 1]) for k in range(BLOCK)]
                group = jnp.where(inside, 0.0, group)
                for k in range(BLOCK):
                    scaled = column[k] * inverse_pivot[k]
                    for m in range(k + 1, BLOCK):
                        column[m] = column[m] - scaled * lower[m, k]
                    group = group - scaled * solved[k]
                work[later : later + BLOCK, :] = group
        if stop < rank:
            panel = work[start:stop, :]
            across = lax.broadcasted_iota(jnp.int32, panel.shape, 1)
            down = lax.broadcasted_iota(jnp.int32, panel.shape, 0) + start
            known = jnp.where((across < stop) & (across > down), 0.0, panel)
            update = three_products(two_terms(panel), two_terms(known), ((0,), (0,)))
            rest = work[stop:, :]
            across = lax.broadcasted_iota(jnp.int32, rest.shape, 1)
            rest = jnp.where((across >= start) & (across < stop), 0.0, rest)
            work[stop:, :] = rest - update[stop:, :]


def finish_kernel(
    place, own, other, fibres, basis, core, current, work, columns, turned, left
):
    rows = own.shape[0]
    first = place[0] == 0
    current[:rows, :] = jnp.where(first, own[...], other[...])
    current[rows:, :] = jnp.where(first, other[...], own[...])
    for top in range(0, current.shape[0], BLOCK):
        some = current[top : top + BLOCK, :]
        current[top : top + BLOCK, :] = some * lax.rsqrt(jnp.sum(some * some, axis=1, keepdims=True))

    def sweep(_, carry):
        before = current[...]
        terms = two_terms(before)
        work[...] = three_products(terms, terms, ((1,), (1,)))
        invert_factor(work, columns)
        across = lax.broadcasted_iota(jnp.int32, work.shape, 1)
        down = lax.broadcasted_iota(jnp.int32, work.shape, 0)
        inverse = jnp.where(across <= down, work[...], 0.0)
        current[...] = exact_dot(inverse, before, ((1,), (0,)))
        return carry

    lax.fori_loop(0, 2, sweep, 0)
    turned[...] = current[...].T
    send = pltpu.make_async_copy(turned, basis, left)
    send.start()
    rows = two_terms(current[...])
    for first in range(0, fibres.shape[1], CHUNK):
        part = slice(first, first + CHUNK)
        core[:, part] = three_products(rows, two_terms(fibres[:, part]))
    send.wait()


def in_vmem(value):
    return pltpu.with_memory_space_constraint(value, pltpu.VMEM)


def finish(core, own, other, fibres):
    rank, length = own.shape[0] * 2, own.shape[1]
    some = fibres.shape[1]
    return pl.pallas_call(
        finish_kernel,
        out_shape=(
            pltpu.HBM((length, rank), jnp.float32),
            pltpu.VMEM((rank, some), jnp.float32),
        ),
        in_specs=[
            pl.BlockSpec(memory_space=pltpu.SMEM),
            pl.BlockSpec(memory_space=pltpu.VMEM),
            pl.BlockSpec(memory_space=pltpu.VMEM),
            pl.BlockSpec(memory_space=pltpu.VMEM),
        ],
        out_specs=(pl.BlockSpec(memory_space=pl.ANY), pl.BlockSpec(memory_space=pltpu.VMEM)),
        scratch_shapes=[
            pltpu.VMEM((rank, length), jnp.float32),
            pltpu.VMEM((rank, rank), jnp.float32),
            pltpu.VMEM((BLOCK * BLOCK, LANES), jnp.float32),
            pltpu.VMEM((length, rank), jnp.float32),
            pltpu.SemaphoreType.DMA,
        ],
        compiler_params=pltpu.CompilerParams(vmem_limit_bytes=16 * 2**20),
    )(
        core[None], in_vmem(own), in_vmem(other), in_vmem(fibres)
    )


def regroup_kernel(snapshots, pieces, arrived):
    members, _, some = pieces.shape
    arrivals = []
    for member in range(members):
        columns = slice(member * some, (member + 1) * some)
        arrivals.append(
            pltpu.make_async_copy(snapshots.at[:, columns], pieces.at[member], arrived.at[member])
        )
        arrivals[-1].start()
    for arrival in arrivals:
        arrival.wait()


def regroup(snapshots, members):
    rows, length = snapshots.shape
    return pl.pallas_call(
        regroup_kernel,
        out_shape=pltpu.VMEM((members, rows, length // members), jnp.float32),
        in_specs=[pl.BlockSpec(memory_space=pl.ANY)],
        out_specs=pl.BlockSpec(memory_space=pltpu.VMEM),
        scratch_shapes=[pltpu.SemaphoreType.DMA((members,))],
        compiler_params=pltpu.CompilerParams(vmem_limit_bytes=4 * 2**20),
    )(pltpu.with_memory_space_constraint(snapshots, pltpu.HBM))


def from_everyone(value, axis):
    copies = jnp.broadcast_to(value, (lax.axis_size(axis), *value.shape))
    return lax.all_to_all(copies, axis, split_axis=0, concat_axis=0, tiled=True)


def half_sums(value, core):
    rows, lanes = value.shape
    tiles = value.reshape(rows // 8, 8, lanes // LANES, LANES).swapaxes(1, 2)
    halves = tiles.reshape(2, -1, 8, LANES)
    swap = [(0, 1), (1, 0)]
    away = lax.dynamic_index_in_dim(halves, 1 - core, 0, keepdims=False)
    kept = lax.dynamic_index_in_dim(halves, core, 0, keepdims=False)
    kept = kept + lax.ppermute(away, "core", swap)
    pieces = kept.reshape(lax.axis_size(COLS), -1, 8, LANES)
    own = lax.all_to_all(pieces, COLS, 0, 0, tiled=True).sum(axis=0)
    own = from_everyone(own, "z").sum(axis=0)
    half = from_everyone(own, COLS)
    other = lax.ppermute(half, "core", swap)
    shape = (rows // 16, lanes // LANES, 8, LANES)
    return [
        part.reshape(shape).swapaxes(1, 2).reshape(rows // 2, lanes) for part in (half, other)
    ]


def lay_out_kernel(groups, whole, left):
    members, _, some = groups.shape
    sends = []
    for member in range(members):
        columns = slice(member * some, (member + 1) * some)
        sends.append(pltpu.make_async_copy(groups.at[member], whole.at[:, columns], left.at[member]))
        sends[-1].start()
    for send in sends:
        send.wait()


def lay_out(groups):
    members, rows, some = groups.shape
    return pl.pallas_call(
        lay_out_kernel,
        out_shape=pltpu.HBM((rows, members * some), jnp.float32),
        in_specs=[pl.BlockSpec(memory_space=pltpu.VMEM)],
        out_specs=pl.BlockSpec(memory_space=pl.ANY),
        scratch_shapes=[pltpu.SemaphoreType.DMA((members,))],
        compiler_params=pltpu.CompilerParams(vmem_limit_bytes=4 * 2**20),
    )(in_vmem(groups))


def shards(snapshots, start_basis):
    pieces = regroup(snapshots, lax.axis_size(MODE))
    core = lax.axis_index("core")
    pieces, core = lax.optimization_barrier((pieces, core))
    fibres = lax.all_to_all(pieces, MODE, 0, 0, tiled=True)
    fibres = fibres.reshape(-1, fibres.shape[-1])
    fibres, start_basis, core = lax.optimization_barrier((fibres, start_basis, core))
    along_cols = close_dot(start_basis, fibres, ((0,), (0,)))
    partial_term = close_dot(along_cols, fibres, ((1,), (1,)))
    basis, core_local = finish(core, *half_sums(partial_term, core), fibres)
    groups = core_local.reshape(lax.axis_size(MODE), -1, core_local.shape[1])
    groups = lax.all_to_all(groups, MODE, 0, 0, tiled=True)
    return (basis, lay_out(groups))


def solution(mesh):
    finer = Mesh(mesh.devices.reshape(8, 2, 4, 4), ("z", "core", "x", "y"))
    return jax.shard_map(
        shards,
        mesh=finer,
        in_specs=(P(MODE, COLS), P()),
        out_specs=(P(), P(MODE, COLS)),
        check_vma=False,
    )
```

```python
import jax
import jax.numpy as jnp
from jax import lax
from jax.experimental import pallas as pl
from jax.experimental.pallas import tpu as pltpu
from jax.sharding import Mesh
from jax.sharding import PartitionSpec as P

MODE = ("z", "core")
COLS = ("x", "y")
PLANE = ("y", "x")
BLOCK = 8
PANEL = 64
CHUNK = 256
LANES = 128


def spread(value):
    return jnp.broadcast_to(value, (BLOCK, LANES))


def exact_dot(left, right, dims):
    return lax.dot_general(
        left,
        right,
        (dims, ((), ())),
        precision=lax.Precision.HIGHEST,
        preferred_element_type=jnp.float32,
    )


def close_dot(left, right, dims):
    return lax.dot_general(
        left,
        right,
        (dims, ((), ())),
        precision=lax.Precision.HIGH,
        preferred_element_type=jnp.float32,
    )


def two_terms(value):
    high = value.astype(jnp.bfloat16)
    return high, (value - high.astype(jnp.float32)).astype(jnp.bfloat16)


def three_products(left, right, dims=((1,), (0,))):
    def product(one, other):
        return lax.dot_general(one, other, (dims, ((), ())), preferred_element_type=jnp.float32)

    left_high, left_low = left
    right_high, right_low = right
    small = product(left_low, right_high) + product(left_high, right_low)
    return small + product(left_high, right_high)


def invert_factor(work, columns):
    rank = work.shape[0]
    lane = lax.broadcasted_iota(jnp.int32, (BLOCK, LANES), 1)
    for start in range(0, rank, PANEL):
        stop = start + PANEL
        for first in range(start, stop, BLOCK):
            lines = [spread(work[first + i : first + i + 1, :]) for i in range(BLOCK)]
            tile = work[first : first + BLOCK, :]
            for j in range(BLOCK):
                columns[BLOCK * j : BLOCK * (j + 1), :] = spread(tile[:, first + j : first + j + 1])
            entry = {
                (i, j): spread(columns[BLOCK * j + i : BLOCK * j + i + 1, :])
                for i in range(BLOCK)
                for j in range(i + 1)
            }
            inside = (lane >= first) & (lane < first + BLOCK)
            lines = [
                jnp.where(inside, (lane == first + i).astype(jnp.float32), line)
                for i, line in enumerate(lines)
            ]
            lower = {}
            inverse_pivot = []
            solved = []
            for j in range(0, BLOCK, 2):
                determinant = entry[j, j] * entry[j + 1, j + 1] - entry[j + 1, j] * entry[j + 1, j]
                inverse_pivot.append(lax.rsqrt(entry[j, j]))
                root = entry[j, j] * inverse_pivot[j]
                inverse_pivot.append(lax.rsqrt(determinant) * root)
                lower[j + 1, j] = entry[j + 1, j] * inverse_pivot[j]
                for i in range(j + 2, BLOCK):
                    lower[i, j] = entry[i, j] * inverse_pivot[j]
                    rest = entry[i, j + 1] - lower[i, j] * lower[j + 1, j]
                    lower[i, j + 1] = rest * inverse_pivot[j + 1]
                for i in range(j + 2, BLOCK):
                    for m in range(i, BLOCK):
                        for k in (j, j + 1):
                            entry[m, i] = entry[m, i] - lower[m, k] * lower[i, k]
                for k in (j, j + 1):
                    solved.append(lines[k] * inverse_pivot[k])
                    for i in range(k + 1, BLOCK):
                        lines[i] = lines[i] - lower[i, k] * solved[k]
                    work[first + k : first + k + 1, :] = solved[k][:1]
            for later in range(first + BLOCK, stop, BLOCK):
                group = work[later : later + BLOCK, :]
                column = [spread(group[:, first + k : first + k + 1]) for k in range(BLOCK)]
                group = jnp.where(inside, 0.0, group)
                for k in range(BLOCK):
                    scaled = column[k] * inverse_pivot[k]
                    for m in range(k + 1, BLOCK):
                        column[m] = column[m] - scaled * lower[m, k]
                    group = group - scaled * solved[k]
                work[later : later + BLOCK, :] = group
        if stop < rank:
            panel = work[start:stop, :]
            across = lax.broadcasted_iota(jnp.int32, panel.shape, 1)
            down = lax.broadcasted_iota(jnp.int32, panel.shape, 0) + start
            known = jnp.where((across < stop) & (across > down), 0.0, panel)
            update = three_products(two_terms(panel), two_terms(known), ((0,), (0,)))
            rest = work[stop:, :]
            across = lax.broadcasted_iota(jnp.int32, rest.shape, 1)
            rest = jnp.where((across >= start) & (across < stop), 0.0, rest)
            work[stop:, :] = rest - update[stop:, :]


def finish_kernel(
    place, own, other, fibres, basis, core, current, work, columns, turned, left
):
    rows = own.shape[0]
    first = place[0] == 0
    current[:rows, :] = jnp.where(first, own[...], other[...])
    current[rows:, :] = jnp.where(first, other[...], own[...])
    for top in range(0, current.shape[0], BLOCK):
        some = current[top : top + BLOCK, :]
        current[top : top + BLOCK, :] = some * lax.rsqrt(jnp.sum(some * some, axis=1, keepdims=True))

    def sweep(_, carry):
        before = current[...]
        terms = two_terms(before)
        work[...] = three_products(terms, terms, ((1,), (1,)))
        invert_factor(work, columns)
        across = lax.broadcasted_iota(jnp.int32, work.shape, 1)
        down = lax.broadcasted_iota(jnp.int32, work.shape, 0)
        inverse = jnp.where(across <= down, work[...], 0.0)
        current[...] = exact_dot(inverse, before, ((1,), (0,)))
        return carry

    lax.fori_loop(0, 2, sweep, 0)
    turned[...] = current[...].T
    send = pltpu.make_async_copy(turned, basis, left)
    send.start()
    rows = two_terms(current[...])
    for first in range(0, fibres.shape[1], CHUNK):
        part = slice(first, first + CHUNK)
        core[:, part] = three_products(rows, two_terms(fibres[:, part]))
    send.wait()


def in_vmem(value):
    return pltpu.with_memory_space_constraint(value, pltpu.VMEM)


def finish(core, own, other, fibres):
    rank, length = own.shape[0] * 2, own.shape[1]
    some = fibres.shape[1]
    return pl.pallas_call(
        finish_kernel,
        out_shape=(
            pltpu.HBM((length, rank), jnp.float32),
            pltpu.VMEM((rank, some), jnp.float32),
        ),
        in_specs=[
            pl.BlockSpec(memory_space=pltpu.SMEM),
            pl.BlockSpec(memory_space=pltpu.VMEM),
            pl.BlockSpec(memory_space=pltpu.VMEM),
            pl.BlockSpec(memory_space=pltpu.VMEM),
        ],
        out_specs=(pl.BlockSpec(memory_space=pl.ANY), pl.BlockSpec(memory_space=pltpu.VMEM)),
        scratch_shapes=[
            pltpu.VMEM((rank, length), jnp.float32),
            pltpu.VMEM((rank, rank), jnp.float32),
            pltpu.VMEM((BLOCK * BLOCK, LANES), jnp.float32),
            pltpu.VMEM((length, rank), jnp.float32),
            pltpu.SemaphoreType.DMA,
        ],
        compiler_params=pltpu.CompilerParams(vmem_limit_bytes=16 * 2**20),
    )(
        core[None], in_vmem(own), in_vmem(other), in_vmem(fibres)
    )


def regroup_kernel(snapshots, pieces, arrived):
    members, _, some = pieces.shape
    arrivals = []
    for member in range(members):
        columns = slice(member * some, (member + 1) * some)
        arrivals.append(
            pltpu.make_async_copy(snapshots.at[:, columns], pieces.at[member], arrived.at[member])
        )
        arrivals[-1].start()
    for arrival in arrivals:
        arrival.wait()


def regroup(snapshots, members):
    rows, length = snapshots.shape
    return pl.pallas_call(
        regroup_kernel,
        out_shape=pltpu.VMEM((members, rows, length // members), jnp.float32),
        in_specs=[pl.BlockSpec(memory_space=pl.ANY)],
        out_specs=pl.BlockSpec(memory_space=pltpu.VMEM),
        scratch_shapes=[pltpu.SemaphoreType.DMA((members,))],
        compiler_params=pltpu.CompilerParams(vmem_limit_bytes=4 * 2**20),
    )(pltpu.with_memory_space_constraint(snapshots, pltpu.HBM))


def from_everyone(value, axis):
    copies = jnp.broadcast_to(value, (lax.axis_size(axis), *value.shape))
    return lax.all_to_all(copies, axis, split_axis=0, concat_axis=0, tiled=True)


def half_sums(value, core):
    rows, lanes = value.shape
    tiles = value.reshape(rows // 8, 8, lanes // LANES, LANES).swapaxes(1, 2)
    halves = tiles.reshape(2, -1, 8, LANES)
    swap = [(0, 1), (1, 0)]
    away = lax.dynamic_index_in_dim(halves, 1 - core, 0, keepdims=False)
    kept = lax.dynamic_index_in_dim(halves, core, 0, keepdims=False)
    kept = kept + lax.ppermute(away, "core", swap)
    pieces = kept.reshape(lax.axis_size(PLANE), -1, 8, LANES)
    own = lax.all_to_all(pieces, PLANE, 0, 0, tiled=True).sum(axis=0)
    own = from_everyone(own, "z").sum(axis=0)
    half = from_everyone(own, PLANE)
    other = lax.ppermute(half, "core", swap)
    shape = (rows // 16, lanes // LANES, 8, LANES)
    return [
        part.reshape(shape).swapaxes(1, 2).reshape(rows // 2, lanes) for part in (half, other)
    ]


def shards(snapshots, start_basis):
    pieces = regroup(snapshots, lax.axis_size(MODE))
    core = lax.axis_index("core")
    pieces, core = lax.optimization_barrier((pieces, core))
    fibres = lax.all_to_all(pieces, MODE, 0, 0, tiled=True)
    fibres = fibres.reshape(-1, fibres.shape[-1])
    fibres, start_basis, core = lax.optimization_barrier((fibres, start_basis, core))
    along_cols = close_dot(start_basis, fibres, ((0,), (0,)))
    partial_term = close_dot(along_cols, fibres, ((1,), (1,)))
    basis, core_local = finish(core, *half_sums(partial_term, core), fibres)
    core_tensor = lax.all_to_all(core_local, MODE, split_axis=0, concat_axis=1, tiled=True)
    return (basis, core_tensor)


def solution(mesh):
    finer = Mesh(mesh.devices.reshape(8, 2, 4, 4), ("z", "core", "x", "y"))
    return jax.shard_map(
        shards,
        mesh=finer,
        in_specs=(P(MODE, COLS), P()),
        out_specs=(P(), P(MODE, COLS)),
        check_vma=False,
    )
```
